32 devices in a mesh: sat: 8 (over z, x), tm: 4 (over y, core).
Axes of the slice: x: 2, y: 2, z: 4, core: 2. Of those that a mesh axis runs over, the one named last changes fastest.
Arguments:
- panels: bfloat16 [64, 32, 64, 128], P('sat', 'tm'), may hold values from -0.3125 to 0.3125
- weights: bfloat16 [64, 32, 64], P('sat', 'tm'), may hold values from 0.19921875 to 5
- pair_members: int32 [32, 2], P('sat'), may hold values from 0 to 63, as said below
- pair_live: int32 [32, 32], P('tm', 'sat'), may hold values 0 or 1
Outputs:
- normal_rows: float32 [12288, 128], P(('sat', 'tm'))
The draws below stay inside these ranges and needn't reach their ends.
Inputs may be any that keep to these rules, and one draw needn't show every extreme that they name: `pair_members`: every satellite is a member of exactly one baseline, and both members of baseline p are satellites whose numbers leave the remainder p // 4 when divided by 8.
All inputs are finite; a program needn't handle non-finite values. No bound on the sum of `pair_live` on one device may be relied on, other than what follows from the above.
Results may differ from the reference program's by a relative error of at most 0.0009.
Values may be sent and summed in bfloat16 or wider, within the bound.
A program may use at most 64 MiB of HBM per device.

```python
import math
import jax
import jax.numpy as jnp
from jax import lax

P_SIZE = 128
K = 64
SAT_DEV = 8
NSAT = 64
NPAIR = 32
NEPB = 32


def draw_pair_members(key, part):
    group_count = SAT_DEV
    scores = jax.random.randint(jax.random.fold_in(key, 29), (group_count, group_count), 0, 1 << 20)
    scores = scores * group_count + jnp.arange(group_count, dtype=jnp.int32)[None, :]
    ordering = jnp.argsort(scores, axis=1).astype(jnp.int32)
    owners = jnp.arange(group_count, dtype=jnp.int32)[:, None]
    members = ordering * group_count + owners
    return members.reshape(NPAIR, 2).astype(jnp.int32)


def touch_ends(values, own_key, low, high):
    dims = values.shape
    spot = [jax.random.randint(jax.random.fold_in(own_key, axis), (), 0, dims[axis]) for axis in range(len(dims))]
    values = values.at[tuple(spot)].set(low)
    longest = dims.index(max(dims))
    spot[longest] = (spot[longest] + 1) % dims[longest]
    return values.at[tuple(spot)].set(high)


def block_levels(rng, extent, cuts, least, largest):
    level, own = 1.0, jax.random.fold_in(rng, 6)
    for axis_at, shards_of in cuts:
        heights = jnp.exp(jax.random.uniform(jax.random.fold_in(own, axis_at), (shards_of,), jnp.float32, least / len(cuts), largest / len(cuts)))
        level = level * jnp.repeat(heights, extent[axis_at] // shards_of).reshape([-1 if axis == axis_at else 1 for axis in range(len(extent))])
    return level


def scatter_about(key, dims, width, bound, pieces=(), kind=jnp.bfloat16):
    entries = width * jax.random.normal(key, dims, jnp.float32)
    if pieces:
        entries = entries * block_levels(key, dims, pieces, -0.22, 0.18)
    return jnp.clip(entries, -bound, bound).astype(kind)


def setup_inputs(seed: int = 0) -> dict:
    key_of = jax.random.split(jax.random.key(seed), 5)
    panels = scatter_about(key_of[0], (NSAT, NEPB, K, P_SIZE), ((1.0 / (NEPB * K)) ** 0.5), 0.3125, ((0, 8), (1, 4)))
    weights = jnp.clip(jnp.exp(math.log(5.0) - 3.2227897 * jax.random.uniform(key_of[1], (NSAT, NEPB, K), jnp.float32) ** block_levels(key_of[1], (NSAT, NEPB, K), ((0, 8), (1, 4)), -0.2, 0.2)), 0.19921875, 5.0).astype(jnp.bfloat16)
    pair_members = draw_pair_members(jax.random.fold_in(key_of[4], 71), 0)
    pair_live = touch_ends((jax.random.randint(key_of[3], (NEPB, NPAIR), 0, 4) < 3).astype(jnp.int32), jax.random.fold_in(key_of[3], 1), 0, 1)
    return dict(panels=panels, weights=weights, pair_members=pair_members, pair_live=pair_live)


def scale_rows(root_weight, panel):
    scaled = (root_weight[:, :, None] * panel.astype(jnp.float32)).astype(jnp.bfloat16)
    scaled = lax.optimization_barrier(scaled)
    return scaled.astype(jnp.float32).reshape(-1, panel.shape[-1])

def gram(left_rows, right_rows):
    return lax.dot_general(left_rows, right_rows, (((0,), (0,)), ((), ())), precision=lax.Precision.HIGHEST, preferred_element_type=jnp.float32)

def pair_blocks(first_panel, second_panel, first_weight, second_weight, live_pair):
    first_value = first_weight.astype(jnp.float32)
    second_value = second_weight.astype(jnp.float32)
    dd_weight = live_pair[:, None] * first_value * second_value / (first_value + second_value)
    root_weight = jnp.sqrt(dd_weight)
    first_scaled = scale_rows(root_weight, first_panel)
    second_scaled = scale_rows(root_weight, second_panel)
    first_gram = gram(first_scaled, first_scaled)
    cross_gram = -gram(first_scaled, second_scaled)
    second_gram = gram(second_scaled, second_scaled)
    return jnp.stack([first_gram, cross_gram, second_gram], axis=0)

def reference(panels, weights, pair_members, pair_live):
    params = panels.shape[-1]

    def one_pair(pair_no):
        first_id = pair_members[pair_no, 0].astype(jnp.int32)
        second_id = pair_members[pair_no, 1].astype(jnp.int32)
        first_panel = lax.dynamic_index_in_dim(panels, first_id, 0, keepdims=False)
        second_panel = lax.dynamic_index_in_dim(panels, second_id, 0, keepdims=False)
        first_weight = lax.dynamic_index_in_dim(weights, first_id, 0, keepdims=False)
        second_weight = lax.dynamic_index_in_dim(weights, second_id, 0, keepdims=False)
        live_pair = lax.dynamic_index_in_dim(pair_live, pair_no, 1, keepdims=False).astype(jnp.float32)
        return pair_blocks(first_panel, second_panel, first_weight, second_weight, live_pair)
    blocks = lax.map(one_pair, jnp.arange(NPAIR, dtype=jnp.int32))
    return blocks.reshape(NPAIR * 3 * params, params)
```

```python
import functools
import jax
import jax.numpy as jnp
from jax import lax
from jax.experimental import pallas as pl
from jax.experimental.pallas import tpu as pltpu
from jax.sharding import PartitionSpec as P

MESH = pl.DeviceIdType.MESH
SHARES = (2, 3, 2, 1)


def chunk_sizes(epochs):
    if epochs < sum(SHARES):
        return [1] * epochs
    edges = [epochs * sum(SHARES[:c]) // sum(SHARES) for c in range(len(SHARES) + 1)]
    return [b - a for a, b in zip(edges, edges[1:])]


def partner(me, k, n):
    place, other = 1, 0
    while place < n:
        other = other + lax.rem(me // place + k // place, 2) * place
        place *= 2
    return other


def send_order(chunks, nsat):
    half = nsat // 2
    return [(c, far, j) for c in chunks for far in (1, 0) for j in range(half)]


def kernel(nsat, ntm, panels, weights, members_hbm, live_hbm, out_ref, *scratch):
    epochs, rows, params = panels.shape[1:]
    sizes = chunk_sizes(epochs)
    count = len(sizes)
    chunks = range(count)
    starts = [sum(sizes[:c]) for c in chunks]
    held, scaled, joined = (scratch[n * count:(n + 1) * count] for n in range(3))
    (heldw, root_ref, members, live_ref, psend, precv, wsend, wrecv, fsend, frecv, lsem,
     sready, tready) = scratch[3 * count:]
    pairs = members.shape[1]
    per_owner = pairs // ntm
    half = nsat // 2
    s = lax.axis_index("sat")
    t = lax.axis_index("tm")
    sat = lambda d: dict(device_id={"sat": d}, device_id_type=MESH)
    tm = lambda d: dict(device_id={"tm": d}, device_id_type=MESH)

    barrier = pltpu.get_barrier_semaphore()
    for d in range(1, nsat):
        @pl.when(d > s)
        def _():
            pl.semaphore_signal(barrier, inc=1, **sat(d))
    for d in range(1, ntm):
        @pl.when(d > t)
        def _():
            pl.semaphore_signal(barrier, inc=1, **tm(d))

    own_panels = [
        pltpu.make_async_copy(panels.at[s, pl.ds(starts[c], sizes[c])], held[c].at[s], lsem.at[c])
        for c in chunks
    ]
    own_weight = pltpu.make_async_copy(weights.at[s], heldw.at[s], lsem.at[count])
    own_members = pltpu.make_async_copy(members_hbm, members, lsem.at[count + 1])
    own_live = pltpu.make_async_copy(live_hbm, live_ref, lsem.at[count + 2])

    @pl.when(s + t > 0)
    def _():
        pl.semaphore_wait(barrier, s + t)
    for d in range(nsat - 1):
        @pl.when(d < s)
        def _():
            pl.semaphore_signal(sready.at[s], inc=1, **sat(d))
    for d in range(ntm - 1):
        @pl.when(d < t)
        def _():
            pl.semaphore_signal(tready.at[t], inc=1, **tm(d))

    def weight_copy(d):
        return pltpu.make_async_remote_copy(
            src_ref=weights.at[d], dst_ref=heldw.at[s], send_sem=wsend.at[d], recv_sem=wrecv.at[s], **sat(d))

    def weight_arrival(d):
        return pltpu.make_async_remote_copy(
            src_ref=weights.at[s], dst_ref=heldw.at[d], send_sem=wsend.at[d], recv_sem=wrecv.at[d], **sat(d))

    def panel_copy(c, d):
        return pltpu.make_async_remote_copy(
            src_ref=panels.at[d, pl.ds(starts[c], sizes[c])], dst_ref=held[c].at[s],
            send_sem=psend.at[c, d], recv_sem=precv.at[c, s], **sat(d))

    def panel_arrival(c, d):
        return pltpu.make_async_remote_copy(
            src_ref=panels.at[s, pl.ds(starts[c], sizes[c])], dst_ref=held[c].at[d],
            send_sem=psend.at[c, d], recv_sem=precv.at[c, d], **sat(d))

    side = s // half
    met = set()
    for c, far, j in send_order(chunks, nsat):
        d = (1 - side if far else side) * half + j
        first = (far, j) not in met
        met.add((far, j))

        def send(c=c, d=d, first=first):
            if first:
                @pl.when(d > s)
                def _():
                    pl.semaphore_wait(sready.at[d], 1)
                weight_copy(d).start()
            panel_copy(c, d).start()

        if far:
            send()
        else:
            pl.when(d != s)(send)
    for copy in (own_members, own_live, own_weight, *own_panels):
        copy.start()

    def others(f):
        for d in range(nsat):
            @pl.when(d != s)
            def _():
                f(d)

    own_live.wait()
    root_ref[...] = jnp.zeros_like(root_ref)
    root_ref[:pairs, :epochs] = live_ref[...].astype(jnp.float32)
    live_all = jnp.transpose(root_ref[:128])[:epochs]
    pair_lane = lax.broadcasted_iota(jnp.int32, live_all.shape, 1)
    offsets = list(range(2, ntm)) + [1, 0]
    slots = [(k, r) for k in offsets for r in range(per_owner)]
    owners = {k: partner(t, k, ntm) for k in offsets}

    own_members.wait()
    own_weight.wait()
    others(lambda d: weight_arrival(d).wait_recv())
    firsts, seconds = [], []
    for n, (k, r) in enumerate(slots):
        pair = owners[k] * per_owner + r
        first, second = members[0, pair] // nsat, members[1, pair] // nsat
        firsts.append(first)
        seconds.append(second)
        u = heldw[first].astype(jnp.float32)
        v = heldw[second].astype(jnp.float32)
        live = jnp.sum(jnp.where(pair_lane == pair, live_all, 0.0), axis=1, keepdims=True)
        root_ref[n * epochs:(n + 1) * epochs, :rows] = jnp.sqrt(live * u * v / (u + v))
    root = jnp.transpose(root_ref[...])

    for d in range(1, ntm):
        @pl.when(d > t)
        def _():
            pl.semaphore_wait(tready.at[d], 1)

    def forward(c, k):
        return pltpu.make_async_remote_copy(
            src_ref=scaled[c].at[k - 1], dst_ref=joined[c].at[k],
            send_sem=fsend.at[c, k], recv_sem=frecv.at[c, k], **tm(owners[k]))

    totals = [None] * per_owner

    def add_joined(c):
        for k in offsets[:-1]:
            forward(c, k).wait_recv()
        for r in range(per_owner):
            if per_owner == 1:
                both = joined[c][...].reshape(ntm * sizes[c] * rows, 2 * params)
            else:
                both = joined[c][:, r].reshape(ntm * sizes[c] * rows, 2 * params)
            term = lax.dot_general(both, both, (((0,), (0,)), ((), ())), preferred_element_type=jnp.float32)
            totals[r] = term if totals[r] is None else totals[r] + term

    for c in chunks:
        own_panels[c].wait()
        others(lambda d: panel_arrival(c, d).wait_recv())
        for n, (k, r) in enumerate(slots):
            into = scaled[c].at[k - 1, r] if k else joined[c].at[0, r]
            for e in range(sizes[c]):
                at = n * epochs + starts[c] + e
                column = root[:rows, at:at + 1]
                here = slice(e * rows, (e + 1) * rows)
                into[here, :params] = (column * held[c][firsts[n], e].astype(jnp.float32)).astype(jnp.bfloat16)
                into[here, params:] = (column * held[c][seconds[n], e].astype(jnp.float32)).astype(jnp.bfloat16)
            if k > 0 and r == per_owner - 1:
                forward(c, k).start()
        if c > 0:
            add_joined(c - 1)
    others(lambda d: weight_copy(d).wait_send())
    for c in chunks:
        others(lambda d: panel_copy(c, d).wait_send())
    add_joined(count - 1)

    for r in range(per_owner):
        base = r * 3 * params
        out_ref[base:base + params] = totals[r][:params, :params]
        out_ref[base + params:base + 2 * params] = -totals[r][:params, params:]
        out_ref[base + 2 * params:base + 3 * params] = totals[r][params:, params:]
    for c in chunks:
        for k in offsets[:-1]:
            forward(c, k).wait_send()


def in_hbm(x):
    return pltpu.with_memory_space_constraint(x, pltpu.HBM)


def per_device(panels, weights, pair_members, pair_live):
    nsat, ntm = lax.axis_size("sat"), lax.axis_size("tm")
    sats, epochs, rows, params = panels.shape
    pairs = pair_members.shape[0]
    per_owner = pairs // ntm
    sizes = chunk_sizes(epochs)
    out_rows = per_owner * 3 * params
    root_rows = -(-pairs * epochs // 128) * 128
    dma = pltpu.SemaphoreType.DMA
    flag = pltpu.SemaphoreType.REGULAR
    hbm = pl.BlockSpec(memory_space=pltpu.HBM)
    return pl.pallas_call(
        functools.partial(kernel, nsat, ntm),
        out_shape=pltpu.VMEM((out_rows, params), jnp.float32),
        in_specs=[hbm] * 4,
        out_specs=pl.BlockSpec(memory_space=pltpu.VMEM),
        scratch_shapes=[
            *[pltpu.VMEM((nsat, size, rows, params), jnp.bfloat16) for size in sizes],
            *[pltpu.VMEM((ntm - 1, per_owner, size * rows, 2 * params), jnp.bfloat16) for size in sizes],
            *[pltpu.VMEM((ntm, per_owner, size * rows, 2 * params), jnp.bfloat16) for size in sizes],
            pltpu.VMEM((nsat, epochs, rows), jnp.bfloat16),
            pltpu.VMEM((root_rows, 128), jnp.float32),
            pltpu.SMEM((2, pairs), jnp.int32),
            pltpu.VMEM((pairs, epochs), jnp.int32),
            dma((len(sizes), nsat)), dma((len(sizes), nsat)),
            dma((nsat,)), dma((nsat,)),
            dma((len(sizes), ntm)), dma((len(sizes), ntm)),
            dma((len(sizes) + 3,)),
            flag((nsat,)), flag((ntm,)),
        ],
        compiler_params=pltpu.CompilerParams(
            collective_id=0, has_side_effects=True, vmem_limit_bytes=40 << 20),
    )(*map(in_hbm, (panels, weights, pair_members.T, pair_live.T)))


def solution(mesh):
    in_specs = (P("sat", "tm", None, None), P("sat", "tm", None), P("sat", None), P("tm", "sat"))
    out_specs = P(("sat", "tm"), None)
    return jax.shard_map(
        per_device, mesh=mesh, in_specs=in_specs, out_specs=out_specs, check_vma=False
    )
```

```python
import functools
import jax
import jax.numpy as jnp
from jax import lax
from jax.experimental import pallas as pl
from jax.experimental.pallas import tpu as pltpu
from jax.sharding import PartitionSpec as P

MESH = pl.DeviceIdType.MESH
SHARES = (2, 1, 1, 1, 1, 1, 1)
LAG = 2
NEAR_FIRST = True
LEAD_UP = (0, 0, 0, 0)
LEAD_DOWN = (1, 0, 0, 0)


def chunk_sizes(epochs):
    if epochs < sum(SHARES):
        return [1] * epochs
    edges = [epochs * sum(SHARES[:c]) // sum(SHARES) for c in range(len(SHARES) + 1)]
    return [b - a for a, b in zip(edges, edges[1:])]


def partner(me, k, n):
    place, other = 1, 0
    while place < n:
        other = other + lax.rem(me // place + k // place, 2) * place
        place *= 2
    return other


def kernel(nsat, ntm, panels, weights, members_hbm, live_hbm, out_ref, *scratch):
    epochs, rows, params = panels.shape[1:]
    sizes = chunk_sizes(epochs)
    count = len(sizes)
    chunks = range(count)
    starts = [sum(sizes[:c]) for c in chunks]
    far_held, scaled, joined = (scratch[n * count:(n + 1) * count] for n in range(3))
    (near_held, nsend, nrecv, heldw, root_ref, members, live_ref, psend, precv, wsend, wrecv, fsend, frecv, lsem,
     sready, tready) = scratch[3 * count:]
    pairs = members.shape[1]
    per_owner = pairs // ntm
    half = nsat // 2
    s = lax.axis_index("sat")
    side = s // half
    t = lax.axis_index("tm")
    sat = lambda d: dict(device_id={"sat": d}, device_id_type=MESH)
    tm = lambda d: dict(device_id={"tm": d}, device_id_type=MESH)

    barrier = pltpu.get_barrier_semaphore()
    for d in range(1, nsat):
        @pl.when(d > s)
        def _():
            pl.semaphore_signal(barrier, inc=1, **sat(d))
    for d in range(1, ntm):
        @pl.when(d > t)
        def _():
            pl.semaphore_signal(barrier, inc=1, **tm(d))

    own_panels = pltpu.make_async_copy(panels.at[s], near_held.at[s % half], lsem.at[0])
    own_weight = pltpu.make_async_copy(weights.at[s], heldw.at[s], lsem.at[1])
    own_members = pltpu.make_async_copy(members_hbm, members, lsem.at[2])
    own_live = pltpu.make_async_copy(live_hbm, live_ref, lsem.at[3])

    for copy in (own_members, own_live, own_weight, own_panels):
        copy.start()

    @pl.when(s + t > 0)
    def _():
        pl.semaphore_wait(barrier, s + t)
    for d in range(nsat - 1):
        @pl.when(d < s)
        def _():
            pl.semaphore_signal(sready.at[s], inc=1, **sat(d))
    for d in range(ntm - 1):
        @pl.when(d < t)
        def _():
            pl.semaphore_signal(tready.at[t], inc=1, **tm(d))

    def weight_copy(d):
        return pltpu.make_async_remote_copy(
            src_ref=weights.at[d], dst_ref=heldw.at[s], send_sem=wsend.at[d], recv_sem=wrecv.at[s], **sat(d))

    def weight_arrival(d):
        return pltpu.make_async_remote_copy(
            src_ref=weights.at[s], dst_ref=heldw.at[d], send_sem=wsend.at[d], recv_sem=wrecv.at[d], **sat(d))

    def far_copy(c, j):
        d = (1 - side) * half + j
        return pltpu.make_async_remote_copy(
            src_ref=panels.at[d, pl.ds(starts[c], sizes[c])], dst_ref=far_held[c].at[s % half],
            send_sem=psend.at[c, j], recv_sem=precv.at[c, s % half], **sat(d))

    def far_arrival(c, j):
        d = (1 - side) * half + j
        return pltpu.make_async_remote_copy(
            src_ref=panels.at[s, pl.ds(starts[c], sizes[c])], dst_ref=far_held[c].at[j],
            send_sem=psend.at[c, j], recv_sem=precv.at[c, j], **sat(d))

    def near_copy(j):
        d = side * half + j
        return pltpu.make_async_remote_copy(
            src_ref=panels.at[d], dst_ref=near_held.at[s % half],
            send_sem=nsend.at[j], recv_sem=nrecv.at[s % half], **sat(d))

    def near_arrival(j):
        d = side * half + j
        return pltpu.make_async_remote_copy(
            src_ref=panels.at[s], dst_ref=near_held.at[j],
            send_sem=nsend.at[j], recv_sem=nrecv.at[j], **sat(d))

    def greet(d):
        @pl.when(d > s)
        def _():
            pl.semaphore_wait(sready.at[d], 1)
        weight_copy(d).start()

    def unless_own(d, f, *args):
        pl.when(d != s)(lambda: f(*args))

    def each_near(f):
        for j in range(half):
            @pl.when(side * half + j != s)
            def _():
                f(j)

    def greet_near(j):
        greet(side * half + j)
        if NEAR_FIRST:
            near_copy(j).start()

    @pl.when(side != 0)
    def _():
        for j in range(half):
            greet(j)
        for j in range(half):
            far_copy(0, j).start()

    each_near(greet_near)

    @pl.when(side == 0)
    def _():
        for j in range(half):
            greet(half + j)
            far_copy(0, j).start()

    if not NEAR_FIRST:
        each_near(lambda j: near_copy(j).start())
    def rest(lead):
        ahead = lambda j: lead[j * len(lead) // half]
        for _, j, c in sorted((c - ahead(j), j, c) for c in range(1, count) for j in range(half)):
            far_copy(c, j).start()

    pl.when(side == 0)(lambda: rest(LEAD_UP))
    pl.when(side != 0)(lambda: rest(LEAD_DOWN))

    def others(f):
        for d in range(nsat):
            @pl.when(d != s)
            def _():
                f(d)

    own_live.wait()
    root_ref[...] = jnp.zeros_like(root_ref)
    root_ref[:pairs, :epochs] = live_ref[...].astype(jnp.float32)
    live_all = jnp.transpose(root_ref[:128])[:epochs]
    pair_lane = lax.broadcasted_iota(jnp.int32, live_all.shape, 1)
    offsets = list(range(2, ntm)) + [1, 0]
    slots = [(k, r) for k in offsets for r in range(per_owner)]
    owners = {k: partner(t, k, ntm) for k in offsets}

    own_members.wait()
    own_weight.wait()
    others(lambda d: weight_arrival(d).wait_recv())
    firsts, seconds = [], []
    for n, (k, r) in enumerate(slots):
        pair = owners[k] * per_owner + r
        first, second = members[0, pair] // nsat, members[1, pair] // nsat
        firsts.append(first)
        seconds.append(second)
        u = heldw[first].astype(jnp.float32)
        v = heldw[second].astype(jnp.float32)
        live = jnp.sum(jnp.where(pair_lane == pair, live_all, 0.0), axis=1, keepdims=True)
        root_ref[n * epochs:(n + 1) * epochs, :rows] = jnp.sqrt(live * u * v / (u + v))
    root = jnp.transpose(root_ref[...])

    for d in range(1, ntm):
        @pl.when(d > t)
        def _():
            pl.semaphore_wait(tready.at[d], 1)

    def forward(c, k):
        return pltpu.make_async_remote_copy(
            src_ref=scaled[c].at[k - 1], dst_ref=joined[c].at[k],
            send_sem=fsend.at[c, k], recv_sem=frecv.at[c, k], **tm(owners[k]))

    totals = [None] * per_owner

    def add_joined(c):
        for k in offsets[:-1]:
            forward(c, k).wait_recv()
        for r in range(per_owner):
            if per_owner == 1:
                both = joined[c][...].reshape(ntm * sizes[c] * rows, 2 * params)
            else:
                both = joined[c][:, r].reshape(ntm * sizes[c] * rows, 2 * params)
            term = lax.dot_general(both, both, (((0,), (0,)), ((), ())), preferred_element_type=jnp.float32)
            totals[r] = term if totals[r] is None else totals[r] + term

    for c in chunks:
        if c == 0:
            own_panels.wait()
            each_near(lambda j: near_arrival(j).wait_recv())
        for j in range(half):
            far_arrival(c, j).wait_recv()
        for n, (k, r) in enumerate(slots):
            into = scaled[c].at[k - 1, r] if k else joined[c].at[0, r]
            for e in range(sizes[c]):
                at = n * epochs + starts[c] + e
                column = root[:rows, at:at + 1]
                here = slice(e * rows, (e + 1) * rows)
                for m, member in enumerate((firsts[n], seconds[n])):
                    near = near_held[member % half, starts[c] + e].astype(jnp.float32)
                    far = far_held[c][member % half, e].astype(jnp.float32)
                    panel = jnp.where(member // half == side, near, far)
                    into[here, m * params:(m + 1) * params] = (column * panel).astype(jnp.bfloat16)
            if k > 0 and r == per_owner - 1:
                forward(c, k).start()
        if c > LAG:
            add_joined(c - 1 - LAG)
    others(lambda d: weight_copy(d).wait_send())
    each_near(lambda j: near_copy(j).wait_send())
    for c in chunks:
        for j in range(half):
            far_copy(c, j).wait_send()
    for c in range(max(count - 1 - LAG, 0), count):
        add_joined(c)

    for r in range(per_owner):
        base = r * 3 * params
        out_ref[base:base + params] = totals[r][:params, :params]
        out_ref[base + params:base + 2 * params] = -totals[r][:params, params:]
        out_ref[base + 2 * params:base + 3 * params] = totals[r][params:, params:]
    for c in chunks:
        for k in offsets[:-1]:
            forward(c, k).wait_send()


def in_hbm(x):
    return pltpu.with_memory_space_constraint(x, pltpu.HBM)


def per_device(panels, weights, pair_members, pair_live):
    nsat, ntm = lax.axis_size("sat"), lax.axis_size("tm")
    sats, epochs, rows, params = panels.shape
    pairs = pair_members.shape[0]
    per_owner = pairs // ntm
    sizes = chunk_sizes(epochs)
    out_rows = per_owner * 3 * params
    root_rows = -(-pairs * epochs // 128) * 128
    dma = pltpu.SemaphoreType.DMA
    flag = pltpu.SemaphoreType.REGULAR
    hbm = pl.BlockSpec(memory_space=pltpu.HBM)
    return pl.pallas_call(
        functools.partial(kernel, nsat, ntm),
        out_shape=pltpu.VMEM((out_rows, params), jnp.float32),
        in_specs=[hbm] * 4,
        out_specs=pl.BlockSpec(memory_space=pltpu.VMEM),
        scratch_shapes=[
            *[pltpu.VMEM((nsat // 2, size, rows, params), jnp.bfloat16) for size in sizes],
            *[pltpu.VMEM((ntm - 1, per_owner, size * rows, 2 * params), jnp.bfloat16) for size in sizes],
            *[pltpu.VMEM((ntm, per_owner, size * rows, 2 * params), jnp.bfloat16) for size in sizes],
            pltpu.VMEM((nsat // 2, epochs, rows, params), jnp.bfloat16),
            dma((nsat // 2,)), dma((nsat // 2,)),
            pltpu.VMEM((nsat, epochs, rows), jnp.bfloat16),
            pltpu.VMEM((root_rows, 128), jnp.float32),
            pltpu.SMEM((2, pairs), jnp.int32),
            pltpu.VMEM((pairs, epochs), jnp.int32),
            dma((len(sizes), nsat // 2)), dma((len(sizes), nsat // 2)),
            dma((nsat,)), dma((nsat,)),
            dma((len(sizes), ntm)), dma((len(sizes), ntm)),
            dma((4,)),
            flag((nsat,)), flag((ntm,)),
        ],
        compiler_params=pltpu.CompilerParams(
            collective_id=0, has_side_effects=True, vmem_limit_bytes=40 << 20),
    )(*map(in_hbm, (panels, weights, pair_members.T, pair_live.T)))


def solution(mesh):
    in_specs = (P("sat", "tm", None, None), P("sat", "tm", None), P("sat", None), P("tm", "sat"))
    out_specs = P(("sat", "tm"), None)
    return jax.shard_map(
        per_device, mesh=mesh, in_specs=in_specs, out_specs=out_specs, check_vma=False
    )
```

```python
import functools
import jax
import jax.numpy as jnp
from jax import lax
from jax.experimental import pallas as pl
from jax.experimental.pallas import tpu as pltpu
from jax.sharding import PartitionSpec as P

MESH = pl.DeviceIdType.MESH
SHARES = (2, 1, 1, 1, 1, 1, 1)
LAG = 2
NEAR_AT = (1, 0, 1, 1)
LEAD_UP = (0, 0, 0, 0)
LEAD_DOWN = (1, 0, 0, 0)


def chunk_sizes(epochs):
    if epochs < sum(SHARES):
        return [1] * epochs
    edges = [epochs * sum(SHARES[:c]) // sum(SHARES) for c in range(len(SHARES) + 1)]
    return [b - a for a, b in zip(edges, edges[1:])]


def partner(me, k, n):
    place, other = 1, 0
    while place < n:
        other = other + lax.rem(me // place + k // place, 2) * place
        place *= 2
    return other


def kernel(nsat, ntm, panels, weights, members_hbm, live_hbm, out_ref, *scratch):
    epochs, rows, params = panels.shape[1:]
    sizes = chunk_sizes(epochs)
    count = len(sizes)
    chunks = range(count)
    starts = [sum(sizes[:c]) for c in chunks]
    far_held, scaled, joined = (scratch[n * count:(n + 1) * count] for n in range(3))
    (near_held, nsend, nrecv, heldw, root_ref, members, live_ref, psend, precv, wsend, wrecv, fsend, frecv, lsem,
     sready, tready) = scratch[3 * count:]
    pairs = members.shape[1]
    per_owner = pairs // ntm
    half = nsat // 2
    s = lax.axis_index("sat")
    side = s // half
    t = lax.axis_index("tm")
    sat = lambda d: dict(device_id={"sat": d}, device_id_type=MESH)
    tm = lambda d: dict(device_id={"tm": d}, device_id_type=MESH)

    barrier = pltpu.get_barrier_semaphore()
    for d in range(1, nsat):
        @pl.when(d > s)
        def _():
            pl.semaphore_signal(barrier, inc=1, **sat(d))
    for d in range(1, ntm):
        @pl.when(d > t)
        def _():
            pl.semaphore_signal(barrier, inc=1, **tm(d))

    own_panels = pltpu.make_async_copy(panels.at[s], near_held.at[s % half], lsem.at[0])
    own_weight = pltpu.make_async_copy(weights.at[s], heldw.at[s], lsem.at[1])
    own_members = pltpu.make_async_copy(members_hbm, members, lsem.at[2])
    own_live = pltpu.make_async_copy(live_hbm, live_ref, lsem.at[3])

    for copy in (own_members, own_live, own_weight, own_panels):
        copy.start()

    @pl.when(s + t > 0)
    def _():
        pl.semaphore_wait(barrier, s + t)
    for d in range(nsat - 1):
        @pl.when(d < s)
        def _():
            pl.semaphore_signal(sready.at[s], inc=1, **sat(d))
    for d in range(ntm - 1):
        @pl.when(d < t)
        def _():
            pl.semaphore_signal(tready.at[t], inc=1, **tm(d))

    def weight_copy(d):
        return pltpu.make_async_remote_copy(
            src_ref=weights.at[d], dst_ref=heldw.at[s], send_sem=wsend.at[d], recv_sem=wrecv.at[s], **sat(d))

    def weight_arrival(d):
        return pltpu.make_async_remote_copy(
            src_ref=weights.at[s], dst_ref=heldw.at[d], send_sem=wsend.at[d], recv_sem=wrecv.at[d], **sat(d))

    def far_copy(c, j):
        d = (1 - side) * half + j
        return pltpu.make_async_remote_copy(
            src_ref=panels.at[d, pl.ds(starts[c], sizes[c])], dst_ref=far_held[c].at[s % half],
            send_sem=psend.at[c, j], recv_sem=precv.at[c, s % half], **sat(d))

    def far_arrival(c, j):
        d = (1 - side) * half + j
        return pltpu.make_async_remote_copy(
            src_ref=panels.at[s, pl.ds(starts[c], sizes[c])], dst_ref=far_held[c].at[j],
            send_sem=psend.at[c, j], recv_sem=precv.at[c, j], **sat(d))

    def near_copy(j):
        d = side * half + j
        return pltpu.make_async_remote_copy(
            src_ref=panels.at[d], dst_ref=near_held.at[s % half],
            send_sem=nsend.at[j], recv_sem=nrecv.at[s % half], **sat(d))

    def near_arrival(j):
        d = side * half + j
        return pltpu.make_async_remote_copy(
            src_ref=panels.at[s], dst_ref=near_held.at[j],
            send_sem=nsend.at[j], recv_sem=nrecv.at[j], **sat(d))

    def greet(d):
        @pl.when(d > s)
        def _():
            pl.semaphore_wait(sready.at[d], 1)
        weight_copy(d).start()

    def unless_own(d, f, *args):
        pl.when(d != s)(lambda: f(*args))

    def each_near(f):
        for j in range(half):
            @pl.when(side * half + j != s)
            def _():
                f(j)

    def send_near():
        each_near(lambda j: near_copy(j).start())

    def greet_near(j):
        greet(side * half + j)

    outer = jnp.where(side == 0, s < half // 2, s >= nsat - half // 2)

    @pl.when(side != 0)
    def _():
        for j in range(half):
            greet(j)
        for j in range(half):
            far_copy(0, j).start()

    each_near(greet_near)

    @pl.when(side == 0)
    def _():
        if NEAR_AT[0] == 0:
            pl.when(outer)(send_near)
        if NEAR_AT[1] == 0:
            pl.when(jnp.logical_not(outer))(send_near)
        for j in range(half):
            greet(half + j)
            far_copy(0, j).start()

    def rest(lead, at):
        ahead = lambda j: lead[j * len(lead) // half]
        order = sorted((c - ahead(j), j, c) for c in range(1, count) for j in range(half))
        for n, (_, j, c) in enumerate(order):
            if n == (at - 1) * half:
                send_near()
            far_copy(c, j).start()

    pl.when((side == 0) & outer)(lambda: rest(LEAD_UP, NEAR_AT[0]))
    pl.when((side == 0) & jnp.logical_not(outer))(lambda: rest(LEAD_UP, NEAR_AT[1]))
    pl.when((side != 0) & jnp.logical_not(outer))(lambda: rest(LEAD_DOWN, NEAR_AT[2]))
    pl.when((side != 0) & outer)(lambda: rest(LEAD_DOWN, NEAR_AT[3]))

    def others(f):
        for d in range(nsat):
            @pl.when(d != s)
            def _():
                f(d)

    own_live.wait()
    root_ref[...] = jnp.zeros_like(root_ref)
    root_ref[:pairs, :epochs] = live_ref[...].astype(jnp.float32)
    live_all = jnp.transpose(root_ref[:128])[:epochs]
    pair_lane = lax.broadcasted_iota(jnp.int32, live_all.shape, 1)
    offsets = list(range(2, ntm)) + [1, 0]
    slots = [(k, r) for k in offsets for r in range(per_owner)]
    owners = {k: partner(t, k, ntm) for k in offsets}

    own_members.wait()
    own_weight.wait()
    others(lambda d: weight_arrival(d).wait_recv())
    firsts, seconds = [], []
    for n, (k, r) in enumerate(slots):
        pair = owners[k] * per_owner + r
        first, second = members[0, pair] // nsat, members[1, pair] // nsat
        firsts.append(first)
        seconds.append(second)
        u = heldw[first].astype(jnp.float32)
        v = heldw[second].astype(jnp.float32)
        live = jnp.sum(jnp.where(pair_lane == pair, live_all, 0.0), axis=1, keepdims=True)
        root_ref[n * epochs:(n + 1) * epochs, :rows] = jnp.sqrt(live * u * v / (u + v))
    root = jnp.transpose(root_ref[...])

    for d in range(1, ntm):
        @pl.when(d > t)
        def _():
            pl.semaphore_wait(tready.at[d], 1)

    def forward(c, k):
        return pltpu.make_async_remote_copy(
            src_ref=scaled[c].at[k - 1], dst_ref=joined[c].at[k],
            send_sem=fsend.at[c, k], recv_sem=frecv.at[c, k], **tm(owners[k]))

    totals = [None] * per_owner

    def add_joined(c):
        for k in offsets[:-1]:
            forward(c, k).wait_recv()
        for r in range(per_owner):
            if per_owner == 1:
                both = joined[c][...].reshape(ntm * sizes[c] * rows, 2 * params)
            else:
                both = joined[c][:, r].reshape(ntm * sizes[c] * rows, 2 * params)
            term = lax.dot_general(both, both, (((0,), (0,)), ((), ())), preferred_element_type=jnp.float32)
            totals[r] = term if totals[r] is None else totals[r] + term

    for c in chunks:
        if c == 0:
            own_panels.wait()
            each_near(lambda j: near_arrival(j).wait_recv())
        for j in range(half):
            far_arrival(c, j).wait_recv()
        for n, (k, r) in enumerate(slots):
            into = scaled[c].at[k - 1, r] if k else joined[c].at[0, r]
            for e in range(sizes[c]):
                at = n * epochs + starts[c] + e
                column = root[:rows, at:at + 1]
                here = slice(e * rows, (e + 1) * rows)
                for m, member in enumerate((firsts[n], seconds[n])):
                    near = near_held[member % half, starts[c] + e].astype(jnp.float32)
                    far = far_held[c][member % half, e].astype(jnp.float32)
                    panel = jnp.where(member // half == side, near, far)
                    into[here, m * params:(m + 1) * params] = (column * panel).astype(jnp.bfloat16)
            if k > 0 and r == per_owner - 1:
                forward(c, k).start()
        if c > LAG:
            add_joined(c - 1 - LAG)
    others(lambda d: weight_copy(d).wait_send())
    each_near(lambda j: near_copy(j).wait_send())
    for c in chunks:
        for j in range(half):
            far_copy(c, j).wait_send()
    for c in range(max(count - 1 - LAG, 0), count):
        add_joined(c)
        if c == count - 2:
            for b in range(count - 1):
                for k in offsets[:-1]:
                    forward(b, k).wait_send()

    for r in range(per_owner):
        base = r * 3 * params
        out_ref[base:base + params] = totals[r][:params, :params]
        out_ref[base + params:base + 2 * params] = -totals[r][:params, params:]
        out_ref[base + 2 * params:base + 3 * params] = totals[r][params:, params:]
    for k in offsets[:-1]:
        forward(count - 1, k).wait_send()


def in_hbm(x):
    return pltpu.with_memory_space_constraint(x, pltpu.HBM)


def per_device(panels, weights, pair_members, pair_live):
    nsat, ntm = lax.axis_size("sat"), lax.axis_size("tm")
    sats, epochs, rows, params = panels.shape
    pairs = pair_members.shape[0]
    per_owner = pairs // ntm
    sizes = chunk_sizes(epochs)
    out_rows = per_owner * 3 * params
    root_rows = -(-pairs * epochs // 128) * 128
    dma = pltpu.SemaphoreType.DMA
    flag = pltpu.SemaphoreType.REGULAR
    hbm = pl.BlockSpec(memory_space=pltpu.HBM)
    return pl.pallas_call(
        functools.partial(kernel, nsat, ntm),
        out_shape=pltpu.VMEM((out_rows, params), jnp.float32),
        in_specs=[hbm] * 4,
        out_specs=pl.BlockSpec(memory_space=pltpu.VMEM),
        scratch_shapes=[
            *[pltpu.VMEM((nsat // 2, size, rows, params), jnp.bfloat16) for size in sizes],
            *[pltpu.VMEM((ntm - 1, per_owner, size * rows, 2 * params), jnp.bfloat16) for size in sizes],
            *[pltpu.VMEM((ntm, per_owner, size * rows, 2 * params), jnp.bfloat16) for size in sizes],
            pltpu.VMEM((nsat // 2, epochs, rows, params), jnp.bfloat16),
            dma((nsat // 2,)), dma((nsat // 2,)),
            pltpu.VMEM((nsat, epochs, rows), jnp.bfloat16),
            pltpu.VMEM((root_rows, 128), jnp.float32),
            pltpu.SMEM((2, pairs), jnp.int32),
            pltpu.VMEM((pairs, epochs), jnp.int32),
            dma((len(sizes), nsat // 2)), dma((len(sizes), nsat // 2)),
            dma((nsat,)), dma((nsat,)),
            dma((len(sizes), ntm)), dma((len(sizes), ntm)),
            dma((4,)),
            flag((nsat,)), flag((ntm,)),
        ],
        compiler_params=pltpu.CompilerParams(
            collective_id=0, has_side_effects=True, vmem_limit_bytes=40 << 20),
    )(*map(in_hbm, (panels, weights, pair_members.T, pair_live.T)))


def solution(mesh):
    in_specs = (P("sat", "tm", None, None), P("sat", "tm", None), P("sat", None), P("tm", "sat"))
    out_specs = P(("sat", "tm"), None)
    return jax.shard_map(
        per_device, mesh=mesh, in_specs=in_specs, out_specs=out_specs, check_vma=False
    )
```

```python
import functools
import jax
import jax.numpy as jnp
from jax import lax
from jax.experimental import pallas as pl
from jax.experimental.pallas import tpu as pltpu
from jax.sharding import PartitionSpec as P

MESH = pl.DeviceIdType.MESH
SHARES = (2, 1, 1, 1, 1, 1, 1)
LAG = 2
NEAR_AT = (1, 0, 1, 1)
LEAD_UP = (0, 0, 0, 0)
LEAD_DOWN = (1, 0, 0, 0)


def chunk_sizes(epochs):
    if epochs < sum(SHARES):
        return [1] * epochs
    edges = [epochs * sum(SHARES[:c]) // sum(SHARES) for c in range(len(SHARES) + 1)]
    return [b - a for a, b in zip(edges, edges[1:])]


def partner(me, k, n):
    place, other = 1, 0
    while place < n:
        other = other + lax.rem(me // place + k // place, 2) * place
        place *= 2
    return other


def kernel(nsat, ntm, panels, weights, members_hbm, live_hbm, out_ref, *scratch):
    epochs, rows, params = panels.shape[1:]
    sizes = chunk_sizes(epochs)
    count = len(sizes)
    chunks = range(count)
    starts = [sum(sizes[:c]) for c in chunks]
    far_held, scaled, joined = (scratch[n * count:(n + 1) * count] for n in range(3))
    (near_held, nsend, nrecv, heldw, root_ref, members, live_ref, psend, precv, wsend, wrecv, fsend, frecv, lsem,
     sready, tready) = scratch[3 * count:]
    pairs = members.shape[1]
    per_owner = pairs // ntm
    half = nsat // 2
    s = lax.axis_index("sat")
    side = s // half
    t = lax.axis_index("tm")
    sat = lambda d: dict(device_id={"sat": d}, device_id_type=MESH)
    tm = lambda d: dict(device_id={"tm": d}, device_id_type=MESH)

    barrier = pltpu.get_barrier_semaphore()
    for d in range(1, nsat):
        @pl.when(d > s)
        def _():
            pl.semaphore_signal(barrier, inc=1, **sat(d))
    for d in range(1, ntm):
        @pl.when(d > t)
        def _():
            pl.semaphore_signal(barrier, inc=1, **tm(d))

    own_panels = pltpu.make_async_copy(panels.at[s], near_held.at[s % half], lsem.at[0])
    own_weight = pltpu.make_async_copy(weights.at[s], heldw.at[s], lsem.at[1])
    own_members = pltpu.make_async_copy(members_hbm, members, lsem.at[2])
    own_live = pltpu.make_async_copy(live_hbm, live_ref, lsem.at[3])

    for copy in (own_members, own_live, own_weight, own_panels):
        copy.start()

    @pl.when(s + t > 0)
    def _():
        pl.semaphore_wait(barrier, s + t)
    for d in range(nsat - 1):
        @pl.when(d < s)
        def _():
            pl.semaphore_signal(sready.at[s], inc=1, **sat(d))
    for d in range(ntm - 1):
        @pl.when(d < t)
        def _():
            pl.semaphore_signal(tready.at[t], inc=1, **tm(d))

    def weight_copy(d):
        return pltpu.make_async_remote_copy(
            src_ref=weights.at[d], dst_ref=heldw.at[s], send_sem=wsend.at[d], recv_sem=wrecv.at[s], **sat(d))

    def weight_arrival(d):
        return pltpu.make_async_remote_copy(
            src_ref=weights.at[s], dst_ref=heldw.at[d], send_sem=wsend.at[d], recv_sem=wrecv.at[d], **sat(d))

    def far_copy(c, j):
        d = (1 - side) * half + j
        return pltpu.make_async_remote_copy(
            src_ref=panels.at[d, pl.ds(starts[c], sizes[c])], dst_ref=far_held[c].at[s % half],
            send_sem=psend.at[c, j], recv_sem=precv.at[c], **sat(d))

    def far_arrival(c, j):
        d = (1 - side) * half + j
        return pltpu.make_async_remote_copy(
            src_ref=panels.at[s, pl.ds(starts[c], sizes[c])], dst_ref=far_held[c].at[j],
            send_sem=psend.at[c, j], recv_sem=precv.at[c], **sat(d))

    def near_copy(j):
        d = side * half + j
        return pltpu.make_async_remote_copy(
            src_ref=panels.at[d], dst_ref=near_held.at[s % half],
            send_sem=nsend.at[j], recv_sem=nrecv.at[s % half], **sat(d))

    def near_arrival(j):
        d = side * half + j
        return pltpu.make_async_remote_copy(
            src_ref=panels.at[s], dst_ref=near_held.at[j],
            send_sem=nsend.at[j], recv_sem=nrecv.at[j], **sat(d))

    def greet(d):
        @pl.when(d > s)
        def _():
            pl.semaphore_wait(sready.at[d], 1)
        weight_copy(d).start()

    def unless_own(d, f, *args):
        pl.when(d != s)(lambda: f(*args))

    def each_near(f):
        for j in range(half):
            @pl.when(side * half + j != s)
            def _():
                f(j)

    def send_near():
        each_near(lambda j: near_copy(j).start())

    def greet_near(j):
        greet(side * half + j)

    outer = jnp.where(side == 0, s < half // 2, s >= nsat - half // 2)

    @pl.when(side != 0)
    def _():
        for j in range(half):
            greet(j)
        for j in range(half):
            far_copy(0, j).start()

    each_near(greet_near)

    @pl.when(side == 0)
    def _():
        if NEAR_AT[0] == 0:
            pl.when(outer)(send_near)
        if NEAR_AT[1] == 0:
            pl.when(jnp.logical_not(outer))(send_near)
        for j in range(half):
            greet(half + j)
            far_copy(0, j).start()

    def rest(lead, at):
        ahead = lambda j: lead[j * len(lead) // half]
        order = sorted((c - ahead(j), j, c) for c in range(1, count) for j in range(half))
        for n, (_, j, c) in enumerate(order):
            if n == (at - 1) * half:
                send_near()
            far_copy(c, j).start()

    pl.when((side == 0) & outer)(lambda: rest(LEAD_UP, NEAR_AT[0]))
    pl.when((side == 0) & jnp.logical_not(outer))(lambda: rest(LEAD_UP, NEAR_AT[1]))
    pl.when((side != 0) & jnp.logical_not(outer))(lambda: rest(LEAD_DOWN, NEAR_AT[2]))
    pl.when((side != 0) & outer)(lambda: rest(LEAD_DOWN, NEAR_AT[3]))

    def others(f):
        for d in range(nsat):
            @pl.when(d != s)
            def _():
                f(d)

    own_live.wait()
    root_ref[...] = jnp.zeros_like(root_ref)
    root_ref[:pairs, :epochs] = live_ref[...].astype(jnp.float32)
    live_all = jnp.transpose(root_ref[:128])[:epochs]
    pair_lane = lax.broadcasted_iota(jnp.int32, live_all.shape, 1)
    offsets = list(range(2, ntm)) + [1, 0]
    slots = [(k, r) for k in offsets for r in range(per_owner)]
    owners = {k: partner(t, k, ntm) for k in offsets}

    own_members.wait()
    own_weight.wait()
    others(lambda d: weight_arrival(d).wait_recv())
    firsts, seconds = [], []
    for n, (k, r) in enumerate(slots):
        pair = owners[k] * per_owner + r
        first, second = members[0, pair] // nsat, members[1, pair] // nsat
        firsts.append(first)
        seconds.append(second)
        u = heldw[first].astype(jnp.float32)
        v = heldw[second].astype(jnp.float32)
        live = jnp.sum(jnp.where(pair_lane == pair, live_all, 0.0), axis=1, keepdims=True)
        root_ref[n * epochs:(n + 1) * epochs, :rows] = jnp.sqrt(live * u * v / (u + v))
    root = jnp.transpose(root_ref[...])

    for d in range(1, ntm):
        @pl.when(d > t)
        def _():
            pl.semaphore_wait(tready.at[d], 1)

    def forward(c, k):
        return pltpu.make_async_remote_copy(
            src_ref=scaled[c].at[k - 1], dst_ref=joined[c].at[k],
            send_sem=fsend.at[c, k], recv_sem=frecv.at[c], **tm(owners[k]))

    totals = [None] * per_owner

    def add_joined(c):
        rest_of = joined[c].at[pl.ds(1, ntm - 1)]
        pltpu.make_async_copy(rest_of, rest_of, frecv.at[c]).wait()
        for r in range(per_owner):
            if per_owner == 1:
                both = joined[c][...].reshape(ntm * sizes[c] * rows, 2 * params)
            else:
                both = joined[c][:, r].reshape(ntm * sizes[c] * rows, 2 * params)
            term = lax.dot_general(both, both, (((0,), (0,)), ((), ())), preferred_element_type=jnp.float32)
            totals[r] = term if totals[r] is None else totals[r] + term

    for c in chunks:
        if c == 0:
            own_panels.wait()
            each_near(lambda j: near_arrival(j).wait_recv())
        pltpu.make_async_copy(far_held[c], far_held[c], precv.at[c]).wait()
        for n, (k, r) in enumerate(slots):
            into = scaled[c].at[k - 1, r] if k else joined[c].at[0, r]
            for e in range(sizes[c]):
                at = n * epochs + starts[c] + e
                column = root[:rows, at:at + 1]
                here = slice(e * rows, (e + 1) * rows)
                for m, member in enumerate((firsts[n], seconds[n])):
                    near = near_held[member % half, starts[c] + e].astype(jnp.float32)
                    far = far_held[c][member % half, e].astype(jnp.float32)
                    panel = jnp.where(member // half == side, near, far)
                    into[here, m * params:(m + 1) * params] = (column * panel).astype(jnp.bfloat16)
            if k > 0 and r == per_owner - 1:
                forward(c, k).start()
        if c > LAG:
            add_joined(c - 1 - LAG)
    others(lambda d: weight_copy(d).wait_send())
    each_near(lambda j: near_copy(j).wait_send())
    for c in chunks:
        for j in range(half):
            far_copy(c, j).wait_send()
    for c in range(max(count - 1 - LAG, 0), count):
        add_joined(c)
        if c == count - 2:
            for b in range(count - 1):
                for k in offsets[:-1]:
                    forward(b, k).wait_send()

    for r in range(per_owner):
        base = r * 3 * params
        out_ref[base:base + params] = totals[r][:params, :params]
        out_ref[base + params:base + 2 * params] = -totals[r][:params, params:]
        out_ref[base + 2 * params:base + 3 * params] = totals[r][params:, params:]
    for k in offsets[:-1]:
        forward(count - 1, k).wait_send()


def in_hbm(x):
    return pltpu.with_memory_space_constraint(x, pltpu.HBM)


def per_device(panels, weights, pair_members, pair_live):
    nsat, ntm = lax.axis_size("sat"), lax.axis_size("tm")
    sats, epochs, rows, params = panels.shape
    pairs = pair_members.shape[0]
    per_owner = pairs // ntm
    sizes = chunk_sizes(epochs)
    out_rows = per_owner * 3 * params
    root_rows = -(-pairs * epochs // 128) * 128
    dma = pltpu.SemaphoreType.DMA
    flag = pltpu.SemaphoreType.REGULAR
    hbm = pl.BlockSpec(memory_space=pltpu.HBM)
    return pl.pallas_call(
        functools.partial(kernel, nsat, ntm),
        out_shape=pltpu.VMEM((out_rows, params), jnp.float32),
        in_specs=[hbm] * 4,
        out_specs=pl.BlockSpec(memory_space=pltpu.VMEM),
        scratch_shapes=[
            *[pltpu.VMEM((nsat // 2, size, rows, params), jnp.bfloat16) for size in sizes],
            *[pltpu.VMEM((ntm - 1, per_owner, size * rows, 2 * params), jnp.bfloat16) for size in sizes],
            *[pltpu.VMEM((ntm, per_owner, size * rows, 2 * params), jnp.bfloat16) for size in sizes],
            pltpu.VMEM((nsat // 2, epochs, rows, params), jnp.bfloat16),
            dma((nsat // 2,)), dma((nsat // 2,)),
            pltpu.VMEM((nsat, epochs, rows), jnp.bfloat16),
            pltpu.VMEM((root_rows, 128), jnp.float32),
            pltpu.SMEM((2, pairs), jnp.int32),
            pltpu.VMEM((pairs, epochs), jnp.int32),
            dma((len(sizes), nsat // 2)), dma((len(sizes),)),
            dma((nsat,)), dma((nsat,)),
            dma((len(sizes), ntm)), dma((len(sizes),)),
            dma((4,)),
            flag((nsat,)), flag((ntm,)),
        ],
        compiler_params=pltpu.CompilerParams(
            collective_id=0, has_side_effects=True, vmem_limit_bytes=40 << 20),
    )(*map(in_hbm, (panels, weights, pair_members.T, pair_live.T)))


def solution(mesh):
    in_specs = (P("sat", "tm", None, None), P("sat", "tm", None), P("sat", None), P("tm", "sat"))
    out_specs = P(("sat", "tm"), None)
    return jax.shard_map(
        per_device, mesh=mesh, in_specs=in_specs, out_specs=out_specs, check_vma=False
    )
```

```python
import functools
import jax
import jax.numpy as jnp
from jax import lax
from jax.experimental import pallas as pl
from jax.experimental.pallas import tpu as pltpu
from jax.sharding import PartitionSpec as P

MESH = pl.DeviceIdType.MESH
SHARES = (2, 1, 1, 1, 1, 1, 1)
LAG = 2
NEAR_AT = (1, 0, 1, 1)
LEAD_UP = (0, 0, 0, 0)
LEAD_DOWN = (1, 0, 0, 0)


def chunk_sizes(epochs):
    if epochs < sum(SHARES):
        return [1] * epochs
    edges = [epochs * sum(SHARES[:c]) // sum(SHARES) for c in range(len(SHARES) + 1)]
    return [b - a for a, b in zip(edges, edges[1:])]


def partner(me, k, n):
    place, other = 1, 0
    while place < n:
        other = other + lax.rem(me // place + k // place, 2) * place
        place *= 2
    return other


def kernel(nsat, ntm, panels, weights, members_hbm, live_hbm, out_ref, *scratch):
    epochs, rows, params = panels.shape[1:]
    sizes = chunk_sizes(epochs)
    count = len(sizes)
    chunks = range(count)
    starts = [sum(sizes[:c]) for c in chunks]
    far_held, scaled, joined = (scratch[n * count:(n + 1) * count] for n in range(3))
    (near_held, nsend, nrecv, heldw, root_ref, members, live_ref, psend, precv, wsend, wrecv, fsend, frecv, lsem,
     sready, tready) = scratch[3 * count:]
    pairs = members.shape[1]
    per_owner = pairs // ntm
    half = nsat // 2
    s = lax.axis_index("sat")
    side = s // half
    t = lax.axis_index("tm")
    sat = lambda d: dict(device_id={"sat": d}, device_id_type=MESH)
    tm = lambda d: dict(device_id={"tm": d}, device_id_type=MESH)

    barrier = pltpu.get_barrier_semaphore()
    for d in range(1, nsat):
        @pl.when(d > s)
        def _():
            pl.semaphore_signal(barrier, inc=1, **sat(d))
    for d in range(1, ntm):
        @pl.when(d > t)
        def _():
            pl.semaphore_signal(barrier, inc=1, **tm(d))

    own_panels = pltpu.make_async_copy(panels.at[s], near_held.at[s % half], lsem.at[0])
    own_weight = pltpu.make_async_copy(weights.at[s], heldw.at[s], lsem.at[1])
    own_members = pltpu.make_async_copy(members_hbm, members, lsem.at[2])
    own_live = pltpu.make_async_copy(live_hbm, live_ref, lsem.at[3])

    for copy in (own_members, own_live, own_weight, own_panels):
        copy.start()

    @pl.when(s + t > 0)
    def _():
        pl.semaphore_wait(barrier, s + t)
    for d in range(nsat - 1):
        @pl.when(d < s)
        def _():
            pl.semaphore_signal(sready.at[s], inc=1, **sat(d))
    for d in range(ntm - 1):
        @pl.when(d < t)
        def _():
            pl.semaphore_signal(tready.at[t], inc=1, **tm(d))

    def weight_copy(d):
        return pltpu.make_async_remote_copy(
            src_ref=weights.at[d], dst_ref=heldw.at[s], send_sem=wsend.at[d], recv_sem=wrecv.at[s], **sat(d))

    def weight_arrival(d):
        return pltpu.make_async_remote_copy(
            src_ref=weights.at[s], dst_ref=heldw.at[d], send_sem=wsend.at[d], recv_sem=wrecv.at[d], **sat(d))

    def far_copy(c, j):
        d = (1 - side) * half + j
        return pltpu.make_async_remote_copy(
            src_ref=panels.at[d, pl.ds(starts[c], sizes[c])], dst_ref=far_held[c].at[s % half],
            send_sem=psend.at[c], recv_sem=precv.at[c], **sat(d))

    def far_arrival(c, j):
        d = (1 - side) * half + j
        return pltpu.make_async_remote_copy(
            src_ref=panels.at[s, pl.ds(starts[c], sizes[c])], dst_ref=far_held[c].at[j],
            send_sem=psend.at[c], recv_sem=precv.at[c], **sat(d))

    def near_copy(j):
        d = side * half + j
        return pltpu.make_async_remote_copy(
            src_ref=panels.at[d], dst_ref=near_held.at[s % half],
            send_sem=nsend.at[j], recv_sem=nrecv.at[s % half], **sat(d))

    def near_arrival(j):
        d = side * half + j
        return pltpu.make_async_remote_copy(
            src_ref=panels.at[s], dst_ref=near_held.at[j],
            send_sem=nsend.at[j], recv_sem=nrecv.at[j], **sat(d))

    def greet(d):
        @pl.when(d > s)
        def _():
            pl.semaphore_wait(sready.at[d], 1)
        weight_copy(d).start()

    def unless_own(d, f, *args):
        pl.when(d != s)(lambda: f(*args))

    def each_near(f):
        for j in range(half):
            @pl.when(side * half + j != s)
            def _():
                f(j)

    def send_near():
        each_near(lambda j: near_copy(j).start())

    def greet_near(j):
        greet(side * half + j)

    outer = jnp.where(side == 0, s < half // 2, s >= nsat - half // 2)

    @pl.when(side != 0)
    def _():
        for j in range(half):
            greet(j)
        for j in range(half):
            far_copy(0, j).start()

    each_near(greet_near)

    @pl.when(side == 0)
    def _():
        if NEAR_AT[0] == 0:
            pl.when(outer)(send_near)
        if NEAR_AT[1] == 0:
            pl.when(jnp.logical_not(outer))(send_near)
        for j in range(half):
            greet(half + j)
            far_copy(0, j).start()

    def rest(lead, at):
        ahead = lambda j: lead[j * len(lead) // half]
        order = sorted((c - ahead(j), j, c) for c in range(1, count) for j in range(half))
        for n, (_, j, c) in enumerate(order):
            if n == (at - 1) * half:
                send_near()
            far_copy(c, j).start()

    pl.when((side == 0) & outer)(lambda: rest(LEAD_UP, NEAR_AT[0]))
    pl.when((side == 0) & jnp.logical_not(outer))(lambda: rest(LEAD_UP, NEAR_AT[1]))
    pl.when((side != 0) & jnp.logical_not(outer))(lambda: rest(LEAD_DOWN, NEAR_AT[2]))
    pl.when((side != 0) & outer)(lambda: rest(LEAD_DOWN, NEAR_AT[3]))

    def others(f):
        for d in range(nsat):
            @pl.when(d != s)
            def _():
                f(d)

    own_live.wait()
    root_ref[...] = jnp.zeros_like(root_ref)
    root_ref[:pairs, :epochs] = live_ref[...].astype(jnp.float32)
    live_all = jnp.transpose(root_ref[:128])[:epochs]
    pair_lane = lax.broadcasted_iota(jnp.int32, live_all.shape, 1)
    offsets = list(range(2, ntm)) + [1, 0]
    slots = [(k, r) for k in offsets for r in range(per_owner)]
    owners = {k: partner(t, k, ntm) for k in offsets}

    own_members.wait()
    own_weight.wait()
    others(lambda d: weight_arrival(d).wait_recv())
    firsts, seconds = [], []
    for n, (k, r) in enumerate(slots):
        pair = owners[k] * per_owner + r
        first, second = members[0, pair] // nsat, members[1, pair] // nsat
        firsts.append(first)
        seconds.append(second)
        u = heldw[first].astype(jnp.float32)
        v = heldw[second].astype(jnp.float32)
        live = jnp.sum(jnp.where(pair_lane == pair, live_all, 0.0), axis=1, keepdims=True)
        root_ref[n * epochs:(n + 1) * epochs, :rows] = jnp.sqrt(live * u * v / (u + v))
    root = jnp.transpose(root_ref[...])

    for d in range(1, ntm):
        @pl.when(d > t)
        def _():
            pl.semaphore_wait(tready.at[d], 1)

    def forward(c, k):
        return pltpu.make_async_remote_copy(
            src_ref=scaled[c].at[k - 1], dst_ref=joined[c].at[k],
            send_sem=fsend.at[c], recv_sem=frecv.at[c], **tm(owners[k]))

    totals = [None] * per_owner

    def add_joined(c):
        rest_of = joined[c].at[pl.ds(1, ntm - 1)]
        pltpu.make_async_copy(rest_of, rest_of, frecv.at[c]).wait()
        for r in range(per_owner):
            if per_owner == 1:
                both = joined[c][...].reshape(ntm * sizes[c] * rows, 2 * params)
            else:
                both = joined[c][:, r].reshape(ntm * sizes[c] * rows, 2 * params)
            term = lax.dot_general(both, both, (((0,), (0,)), ((), ())), preferred_element_type=jnp.float32)
            totals[r] = term if totals[r] is None else totals[r] + term

    for c in chunks:
        if c == 0:
            own_panels.wait()
            each_near(lambda j: near_arrival(j).wait_recv())
        pltpu.make_async_copy(far_held[c], far_held[c], precv.at[c]).wait()
        for n, (k, r) in enumerate(slots):
            into = scaled[c].at[k - 1, r] if k else joined[c].at[0, r]
            for e in range(sizes[c]):
                at = n * epochs + starts[c] + e
                column = root[:rows, at:at + 1]
                here = slice(e * rows, (e + 1) * rows)
                for m, member in enumerate((firsts[n], seconds[n])):
                    near = near_held[member % half, starts[c] + e].astype(jnp.float32)
                    far = far_held[c][member % half, e].astype(jnp.float32)
                    panel = jnp.where(member // half == side, near, far)
                    into[here, m * params:(m + 1) * params] = (column * panel).astype(jnp.bfloat16)
            if k > 0 and r == per_owner - 1:
                forward(c, k).start()
        if c > LAG:
            add_joined(c - 1 - LAG)
    others(lambda d: weight_copy(d).wait_send())
    each_near(lambda j: near_copy(j).wait_send())
    for c in chunks:
        pltpu.make_async_copy(far_held[c], far_held[c], psend.at[c]).wait()
    for c in range(max(count - 1 - LAG, 0), count):
        add_joined(c)
        if c == count - 2:
            for b in range(count - 1):
                pltpu.make_async_copy(scaled[b], scaled[b], fsend.at[b]).wait()

    for r in range(per_owner):
        base = r * 3 * params
        out_ref[base:base + params] = totals[r][:params, :params]
        out_ref[base + params:base + 2 * params] = -totals[r][:params, params:]
        out_ref[base + 2 * params:base + 3 * params] = totals[r][params:, params:]
    pltpu.make_async_copy(scaled[-1], scaled[-1], fsend.at[count - 1]).wait()


def in_hbm(x):
    return pltpu.with_memory_space_constraint(x, pltpu.HBM)


def per_device(panels, weights, pair_members, pair_live):
    nsat, ntm = lax.axis_size("sat"), lax.axis_size("tm")
    sats, epochs, rows, params = panels.shape
    pairs = pair_members.shape[0]
    per_owner = pairs // ntm
    sizes = chunk_sizes(epochs)
    out_rows = per_owner * 3 * params
    root_rows = -(-pairs * epochs // 128) * 128
    dma = pltpu.SemaphoreType.DMA
    flag = pltpu.SemaphoreType.REGULAR
    hbm = pl.BlockSpec(memory_space=pltpu.HBM)
    return pl.pallas_call(
        functools.partial(kernel, nsat, ntm),
        out_shape=pltpu.VMEM((out_rows, params), jnp.float32),
        in_specs=[hbm] * 4,
        out_specs=pl.BlockSpec(memory_space=pltpu.VMEM),
        scratch_shapes=[
            *[pltpu.VMEM((nsat // 2, size, rows, params), jnp.bfloat16) for size in sizes],
            *[pltpu.VMEM((ntm - 1, per_owner, size * rows, 2 * params), jnp.bfloat16) for size in sizes],
            *[pltpu.VMEM((ntm, per_owner, size * rows, 2 * params), jnp.bfloat16) for size in sizes],
            pltpu.VMEM((nsat // 2, epochs, rows, params), jnp.bfloat16),
            dma((nsat // 2,)), dma((nsat // 2,)),
            pltpu.VMEM((nsat, epochs, rows), jnp.bfloat16),
            pltpu.VMEM((root_rows, 128), jnp.float32),
            pltpu.SMEM((2, pairs), jnp.int32),
            pltpu.VMEM((pairs, epochs), jnp.int32),
            dma((len(sizes),)), dma((len(sizes),)),
            dma((nsat,)), dma((nsat,)),
            dma((len(sizes),)), dma((len(sizes),)),
            dma((4,)),
            flag((nsat,)), flag((ntm,)),
        ],
        compiler_params=pltpu.CompilerParams(
            collective_id=0, has_side_effects=True, vmem_limit_bytes=40 << 20),
    )(*map(in_hbm, (panels, weights, pair_members.T, pair_live.T)))


def solution(mesh):
    in_specs = (P("sat", "tm", None, None), P("sat", "tm", None), P("sat", None), P("tm", "sat"))
    out_specs = P(("sat", "tm"), None)
    return jax.shard_map(
        per_device, mesh=mesh, in_specs=in_specs, out_specs=out_specs, check_vma=False
    )
```
